256 devices in a mesh: tm: 32 (over y, x, core), space: 8 (over z).
Axes of the slice: x: 4, y: 4, z: 8, core: 2. Of those that a mesh axis runs over, the one named last changes fastest.
Arguments:
- frames_in: bfloat16 [32, 128, 128, 256], P('tm', 'space'), may hold values from -6 to 6
- w_input: bfloat16 [3, 3, 256, 256], replicated, may hold values from -0.125 to 0.125
- decay_rate: float32 [128], replicated, may hold values from 0.001 to 0.2
- phase: float32 [128], replicated, may hold values from -3.140625 to 3.140625
- w_output: bfloat16 [3, 3, 256, 256], replicated, may hold values from -0.125 to 0.125
Outputs:
- frames_out: bfloat16 [32, 128, 128, 256], P('tm', 'space')
The draws below stay inside these ranges and needn't reach their ends.
All inputs are finite; a program needn't handle non-finite values.
Results may differ from the reference program's by a relative error of at most 0.0029.
Values may be sent and summed in bfloat16 or wider, within the bound.
A program may use at most 192 MiB of HBM per device.

```python
import math
import jax
import jax.numpy as jnp
from jax import lax

C = 256
P_SIZE = 128
HEIGHT = 128
W = 128
FRAMES = 32


def shard_levels(stream_key, extent, cuts, least, largest):
    level = 1.0
    for position, shards_of in cuts:
        steps = jax.random.uniform(jax.random.fold_in(jax.random.fold_in(stream_key, 6), position), (shards_of,), jnp.float32, least / len(cuts), largest / len(cuts))
        level = level * jnp.repeat(jnp.exp(steps), extent[position] // shards_of).reshape((-1,) + (1,) * (len(extent) - 1 - position))
    return level


def gaussian(stream_key, extent, spread, most, cuts=(), dtype=jnp.bfloat16):
    values = spread * jax.random.normal(stream_key, extent, jnp.float32)
    if cuts:
        values = values * shard_levels(stream_key, extent, cuts, -0.22, 0.18)
    return jnp.clip(values, -most, most).astype(dtype)


def setup_inputs(seed: int = 0) -> dict:
    key_list = jax.random.split(jax.random.key(seed), 6)
    frames_in = gaussian(key_list[0], (FRAMES, HEIGHT, W, C), 1.0, 6.0, ((0, 32), (1, 8)))
    w_input = gaussian(key_list[1], (3, 3, C, 2 * P_SIZE), (9 * C) ** -0.5, 0.125)
    decay_rate = jnp.clip(jnp.exp(jax.random.uniform(key_list[2], (P_SIZE,), jnp.float32, math.log(0.001), math.log(0.2))), 0.001, 0.2)
    phase = jnp.clip(jax.random.uniform(key_list[3], (P_SIZE,), jnp.float32, -3.140625, 3.140625), -3.140625, 3.140625)
    w_output = gaussian(key_list[4], (3, 3, 2 * P_SIZE, C), (18 * P_SIZE) ** -0.5, 0.125)
    return dict(frames_in=frames_in, w_input=w_input, decay_rate=decay_rate, phase=phase, w_output=w_output)


def convolve(data, kernel):
    return lax.conv_general_dilated(data.astype(jnp.float32), kernel.astype(jnp.float32), (1, 1), ((1, 1), (1, 1)), dimension_numbers=('NHWC', 'HWIO', 'NHWC'), precision=lax.Precision.HIGHEST)

def reference(frames_in, w_input, decay_rate, phase, w_output):
    drive = convolve(frames_in, w_input)
    magnitude = jnp.exp(-decay_rate)
    lam_re = magnitude * jnp.cos(phase)
    lam_im = magnitude * jnp.sin(phase)
    factor = jnp.sqrt(1.0 - magnitude * magnitude)
    feed = drive * jnp.concatenate([factor, factor])

    def advance(carry, item):
        prev_re, prev_im = carry
        new_re = lam_re * prev_re - lam_im * prev_im + item[..., :P_SIZE]
        new_im = lam_re * prev_im + lam_im * prev_re + item[..., P_SIZE:]
        return ((new_re, new_im), jnp.concatenate([new_re, new_im], axis=-1).astype(jnp.bfloat16))
    start = jnp.zeros(feed.shape[1:3] + (P_SIZE,), jnp.float32)
    final, state_b = lax.scan(advance, (start, start), feed)
    mixed = convolve(state_b, w_output)
    return (frames_in.astype(jnp.float32) + jax.nn.gelu(mixed, approximate=False)).astype(jnp.bfloat16)
```

```python
import functools

import jax
import jax.numpy as jnp
from jax import lax
from jax.experimental import pallas as pl
from jax.experimental.pallas import tpu as pltpu
from jax.sharding import PartitionSpec as P

MESH = pl.DeviceIdType.MESH
NC = 4
SCALE = 16384.0
F32 = jnp.float32
BF16 = jnp.bfloat16


def encode(v):
    return ((v * jnp.abs(v)) * (v * v)).astype(BF16)


def decode(code):
    w = code.astype(F32)
    root = jnp.sqrt(jnp.sqrt(jnp.abs(w)))
    return jnp.where(w < 0, -root, root)


def times(a, b):
    return (a[0] * b[0] - a[1] * b[1], a[0] * b[1] + a[1] * b[0])


def plus(a, b):
    return (a[0] + b[0], a[1] + b[1])


def kernel(
    chips, nz,
    x_hbm, w1_hbm, w2_hbm, decay_ref, phase_ref,
    o_hbm,
    xs, w1, w2, halo, taps, f_own, f_par, a_out, a_in, c_out, c_in, st, st_oth, ov,
    ld_sem, o_sem, hx_s, hx_r, f_s, f_r, a_s, a_r, c_s, c_r, s_s, s_r, hs_s, hs_r,
):
    t, z = lax.axis_index("tm"), lax.axis_index("space")
    core = lax.rem(t, 2)
    chip = t // 2
    mate = t + 1 - 2 * core
    per = 256 // chips
    low, high = z > 0, z < nz - 1

    def peer(d):
        return lax.rem(chip + d, chips)

    def remote(src, dst, send, recv, tm, zz):
        return pltpu.make_async_remote_copy(
            src_ref=src, dst_ref=dst, send_sem=send, recv_sem=recv,
            device_id=(tm, zz), device_id_type=MESH,
        )

    barrier = pltpu.get_barrier_semaphore()

    def greet(tm, zz):
        pl.semaphore_signal(barrier, inc=1, device_id=(tm, zz), device_id_type=MESH)

    greet(mate, z)

    @pl.when(low)
    def _():
        greet(t, z - 1)

    @pl.when(high)
    def _():
        greet(t, z + 1)

    @pl.when(jnp.logical_and(low, core == 0))
    def _():
        greet(mate, z - 1)

    @pl.when(jnp.logical_and(high, core == 1))
    def _():
        greet(mate, z + 1)

    @pl.loop(1, chips)
    def _(d):
        greet(2 * peer(d) + core, z)

    load_x = pltpu.make_async_copy(x_hbm, xs, ld_sem.at[0])
    load_1 = pltpu.make_async_copy(w1_hbm, w1, ld_sem.at[1])
    load_2 = pltpu.make_async_copy(w2_hbm, w2, ld_sem.at[2])
    load_x.start()
    load_1.start()
    load_2.start()

    decay, phase = decay_ref[...], phase_ref[...]
    mag = jnp.exp(-decay)
    lam = (mag * jnp.cos(phase), mag * jnp.sin(phase))
    lam2 = times(lam, lam)
    factor = jnp.sqrt(1.0 - mag * mag) * SCALE
    factor = jnp.concatenate([factor, factor], axis=1)

    def base(half, i):
        return jnp.where(half == 0, 6 - 2 * i, 8 + 2 * i)

    def spread(row, slot):
        v = row.astype(F32)
        at = lax.broadcasted_iota(jnp.int32, v.shape, 0)
        left = jnp.where(at == 0, 0.0, pltpu.roll(v, 1, 0))
        right = jnp.where(at == 127, 0.0, pltpu.roll(v, 127, 0))
        taps[slot, :, 0:256] = left.astype(BF16)
        taps[slot, :, 256:512] = row
        taps[slot, :, 512:768] = right.astype(BF16)

    def conv(w, row):
        acc = None
        for dy in range(3):
            part = jnp.dot(
                taps[pl.ds(row + dy, 2)].reshape(256, 768), w[dy],
                preferred_element_type=F32,
            )
            acc = part if acc is None else acc + part
        return acc

    def drive(i):
        @pl.loop(0, 2)
        def _(n):
            row = base(jnp.where(n == 0, 1 - core, core), i)
            f_own[pl.ds(row, 2)] = (conv(w1, row) * factor).reshape(2, 128, 256)

    def feed_copy(i):
        rows = pl.ds(base(1 - core, i), 2)
        return remote(f_own.at[rows], f_par.at[i], f_s.at[i], f_r.at[i], mate, z)

    def a_copy(i, d):
        j = peer(d)
        return remote(
            a_out.at[i, pl.ds(pl.multiple_of(j * per, per), per)], a_in.at[i, chip],
            a_s.at[i, j], a_r.at[i, chip], 2 * j + core, z,
        )

    def a_landed(i, d):
        j = peer(d)
        return remote(a_in.at[i, j], a_in.at[i, j], a_s.at[i, j], a_r.at[i, j], 2 * j + core, z)

    def c_copy(i, d):
        j = peer(d)
        return remote(
            c_out.at[i, j], c_in.at[i, pl.ds(pl.multiple_of(chip * per, per), per)],
            c_s.at[i, j], c_r.at[i, chip], 2 * j + core, z,
        )

    def c_landed(i, d):
        j = peer(d)
        there = c_in.at[i, pl.ds(pl.multiple_of(j * per, per), per)]
        return remote(there, there, c_s.at[i, j], c_r.at[i, j], 2 * j + core, z)

    def both_feeds(i, row, r, sub):
        mine = f_own[row + r, sub]
        other = f_par[i, r, sub]
        first = jnp.where(core == 0, mine, other)
        second = jnp.where(core == 0, other, mine)
        return (first[:, :128], first[:, 128:]), (second[:, :128], second[:, 128:])

    def aggregate(i):
        feed_copy(i).wait_recv()
        row = base(core, i)

        @pl.loop(0, 4)
        def _(n):
            r, q = n // 2, lax.rem(n, 2)
            sub = pl.ds(pl.multiple_of(q * 64, 64), 64)
            first, second = both_feeds(i, row, r, sub)
            total = plus(times(lam, first), second)
            out = pl.ds(pl.multiple_of(n * 64, 64), 64)
            a_out[i, out, 0:128] = encode(total[0])
            a_out[i, out, 128:256] = encode(total[1])

        @pl.loop(1, chips)
        def _(d):
            a_copy(i, d).start()

        a_in[i, chip] = a_out[i, pl.ds(pl.multiple_of(chip * per, per), per)]

    def scan(i):
        @pl.loop(1, chips)
        def _(d):
            a_landed(i, d).wait_recv()

        carry = (jnp.zeros((per, 128), F32), jnp.zeros((per, 128), F32))
        for k in range(chips):
            c_out[i, k, :, 0:128] = encode(carry[0])
            c_out[i, k, :, 128:256] = encode(carry[1])
            if k < chips - 1:
                got = (decode(a_in[i, k, :, 0:128]), decode(a_in[i, k, :, 128:256]))
                carry = plus(times(lam2, carry), got)

        @pl.loop(1, chips)
        def _(d):
            c_copy(i, d).start()

        c_in[i, pl.ds(pl.multiple_of(chip * per, per), per)] = c_out[i, chip]

    def mate_copy(i):
        rows = pl.ds(1 + base(core, i), 2)
        return remote(st_oth.at[i], st.at[rows], s_s.at[i], s_r.at[i], mate, z)

    def mate_landed(i):
        rows = pl.ds(1 + base(1 - core, i), 2)
        return remote(st.at[rows], st.at[rows], s_s.at[i], s_r.at[i], mate, z)

    def states(i):
        @pl.loop(1, chips)
        def _(d):
            c_landed(i, d).wait_recv()

        row = base(core, i)

        @pl.loop(0, 4)
        def _(n):
            r, q = n // 2, lax.rem(n, 2)
            sub = pl.ds(pl.multiple_of(q * 64, 64), 64)
            first, second = both_feeds(i, row, r, sub)
            took = pl.ds(pl.multiple_of(n * 64, 64), 64)
            carry = (decode(c_in[i, took, 0:128]), decode(c_in[i, took, 128:256]))
            s0 = plus(times(lam, carry), first)
            s1 = plus(times(lam, s0), second)
            for p in range(2):
                lanes = slice(128 * p, 128 * p + 128)
                own = jnp.where(core == 0, s0[p], s1[p]) * (1.0 / SCALE)
                oth = jnp.where(core == 0, s1[p], s0[p]) * (1.0 / SCALE)
                st[1 + row + r, sub, lanes] = own.astype(BF16)
                st_oth[i, r, sub, lanes] = oth.astype(BF16)

        mate_copy(i).start()

    def spread_states(half, i):
        row = base(half, i)

        @pl.loop(0, 2)
        def _(r):
            spread(st[1 + row + r], 1 + row + r)

    def out_copy(half, i):
        rows = pl.ds(base(half, i), 2)
        return pltpu.make_async_copy(ov.at[rows], o_hbm.at[rows], o_sem.at[half, i])

    def finish(i):
        @pl.loop(0, 2)
        def _(half):
            row = base(half, i)
            mixed = conv(w2, row).reshape(2, 128, 256)
            gelu = 0.5 * mixed * (1.0 + lax.erf(mixed * (0.5 ** 0.5)))
            ov[pl.ds(row, 2)] = (xs[pl.ds(row, 2)].astype(F32) + gelu).astype(BF16)
            out_copy(half, i).start()

    load_x.wait()

    @pl.loop(0, 16)
    def _(r):
        spread(xs[r], 1 + r)

    load_1.wait()
    drive(0)

    pl.semaphore_wait(
        barrier,
        chips + low.astype(jnp.int32) + high.astype(jnp.int32)
        + jnp.where(core == 0, low.astype(jnp.int32), high.astype(jnp.int32)),
    )

    up = remote(xs.at[0], halo.at[1], hx_s.at[0], hx_r.at[1], t, z - 1)
    down = remote(xs.at[15], halo.at[0], hx_s.at[1], hx_r.at[0], t, z + 1)
    from_up = remote(halo.at[0], halo.at[0], hx_s.at[1], hx_r.at[0], t, z - 1)
    from_down = remote(halo.at[1], halo.at[1], hx_s.at[0], hx_r.at[1], t, z + 1)

    feed_copy(0).start()

    @pl.when(low)
    def _():
        up.start()

    @pl.when(high)
    def _():
        down.start()

    @pl.loop(1, NC - 1)
    def _(i):
        drive(i)
        feed_copy(i).start()
        aggregate(i - 1)

    def edges(first, second):
        @pl.when(low)
        def _():
            first()

        @pl.when(jnp.logical_not(low))
        def _():
            taps[0] = jnp.zeros((128, 768), BF16)

        @pl.when(high)
        def _():
            second()

        @pl.when(jnp.logical_not(high))
        def _():
            taps[17] = jnp.zeros((128, 768), BF16)

    def halo_first():
        from_up.wait_recv()
        spread(halo[0], 0)

    def halo_second():
        from_down.wait_recv()
        spread(halo[1], 17)

    edges(halo_first, halo_second)
    drive(NC - 1)
    feed_copy(NC - 1).start()
    aggregate(NC - 2)
    aggregate(NC - 1)

    @pl.loop(0, NC)
    def _(i):
        scan(i)

    last = NC - 1
    own_up = remote(st.at[1], st.at[17], hs_s.at[0], hs_r.at[1], t, z - 1)
    oth_up = remote(st_oth.at[last, 0], st.at[17], hs_s.at[1], hs_r.at[1], mate, z - 1)
    own_down = remote(st.at[16], st.at[0], hs_s.at[0], hs_r.at[0], t, z + 1)
    oth_down = remote(st_oth.at[last, 1], st.at[0], hs_s.at[1], hs_r.at[0], mate, z + 1)
    state_up = remote(st.at[0], st.at[0], hs_s.at[0], hs_r.at[0], t, z - 1)
    state_down = remote(st.at[17], st.at[17], hs_s.at[0], hs_r.at[1], t, z + 1)
    sends_up = jnp.logical_and(core == 0, low)
    sends_down = jnp.logical_and(core == 1, high)

    load_2.wait()
    states(0)
    spread_states(core, 0)
    states(1)
    spread_states(core, 1)
    mate_landed(0).wait_recv()
    spread_states(1 - core, 0)
    states(2)
    spread_states(core, 2)
    mate_landed(1).wait_recv()
    spread_states(1 - core, 1)
    finish(0)
    states(3)

    @pl.when(sends_up)
    def _():
        own_up.start()
        oth_up.start()

    @pl.when(sends_down)
    def _():
        own_down.start()
        oth_down.start()

    spread_states(core, 3)
    mate_landed(2).wait_recv()
    spread_states(1 - core, 2)
    finish(1)
    mate_landed(3).wait_recv()
    spread_states(1 - core, 3)
    finish(2)

    def state_first():
        state_up.wait_recv()
        spread(st[0], 0)

    def state_second():
        state_down.wait_recv()
        spread(st[17], 17)

    edges(state_first, state_second)
    finish(3)

    @pl.when(low)
    def _():
        up.wait_send()

    @pl.when(high)
    def _():
        down.wait_send()

    @pl.when(sends_up)
    def _():
        own_up.wait_send()
        oth_up.wait_send()

    @pl.when(sends_down)
    def _():
        own_down.wait_send()
        oth_down.wait_send()

    @pl.loop(0, NC)
    def _(i):
        feed_copy(i).wait_send()
        mate_copy(i).wait_send()

        @pl.loop(1, chips)
        def _(d):
            a_copy(i, d).wait_send()
            c_copy(i, d).wait_send()

        out_copy(0, i).wait()
        out_copy(1, i).wait()


def solution(mesh):
    chips, nz = mesh.shape["tm"] // 2, mesh.shape["space"]
    per = 256 // chips
    any_spec = pl.BlockSpec(memory_space=pl.ANY)
    vmem_spec = pl.BlockSpec(memory_space=pltpu.VMEM)
    dma = pltpu.SemaphoreType.DMA

    def on_device(frames_in, w_input, decay_rate, phase, w_output):
        out = pl.pallas_call(
            functools.partial(kernel, chips, nz),
            out_shape=jax.ShapeDtypeStruct((16, 128, 256), BF16),
            in_specs=[any_spec, any_spec, any_spec, vmem_spec, vmem_spec],
            out_specs=any_spec,
            scratch_shapes=[
                pltpu.VMEM((16, 128, 256), BF16),
                pltpu.VMEM((3, 768, 256), BF16),
                pltpu.VMEM((3, 768, 256), BF16),
                pltpu.VMEM((2, 128, 256), BF16),
                pltpu.VMEM((18, 128, 768), BF16),
                pltpu.VMEM((16, 128, 256), F32),
                pltpu.VMEM((NC, 2, 128, 256), F32),
                pltpu.VMEM((NC, 256, 256), BF16),
                pltpu.VMEM((NC, chips, per, 256), BF16),
                pltpu.VMEM((NC, chips, per, 256), BF16),
                pltpu.VMEM((NC, 256, 256), BF16),
                pltpu.VMEM((18, 128, 256), BF16),
                pltpu.VMEM((NC, 2, 128, 256), BF16),
                pltpu.VMEM((16, 128, 256), BF16),
                dma((3,)), dma((2, NC)), dma((2,)), dma((2,)), dma((NC,)), dma((NC,)),
                dma((NC, chips)), dma((NC, chips)), dma((NC, chips)), dma((NC, chips)),
                dma((NC,)), dma((NC,)), dma((2,)), dma((2,)),
            ],
            compiler_params=pltpu.CompilerParams(
                collective_id=0, has_side_effects=True, vmem_limit_bytes=48 * 1024 * 1024
            ),
            name="convs5",
        )(
            frames_in[0], w_input.reshape(3, 768, 256), w_output.reshape(3, 768, 256),
            decay_rate.reshape(1, 128), phase.reshape(1, 128),
        )
        return out[None]

    in_specs = (P("tm", "space", None, None), P(), P(), P(), P())
    return jax.shard_map(
        on_device, mesh=mesh, in_specs=in_specs,
        out_specs=P("tm", "space", None, None), check_vma=False,
    )
```

```python
import functools

import jax
import jax.numpy as jnp
from jax import lax
from jax.experimental import pallas as pl
from jax.experimental.pallas import tpu as pltpu
from jax.sharding import PartitionSpec as P

MESH = pl.DeviceIdType.MESH
NC = 4
SCALE = 16384.0
F32 = jnp.float32
BF16 = jnp.bfloat16


def encode(v):
    return ((v * jnp.abs(v)) * (v * v)).astype(BF16)


def decode(code):
    w = code.astype(F32)
    root = jnp.sqrt(jnp.sqrt(jnp.abs(w)))
    return jnp.where(w < 0, -root, root)


def times(a, b):
    return (a[0] * b[0] - a[1] * b[1], a[0] * b[1] + a[1] * b[0])


def plus(a, b):
    return (a[0] + b[0], a[1] + b[1])


def kernel(
    chips, nz,
    x_hbm, w1_hbm, w2_hbm, decay_hbm, phase_hbm,
    ov,
    xs, w1, w2, rates, halo, taps, f_own, f_par, a_out, a_in, c_out, c_in, st, st_oth,
    ld_sem, hx_s, hx_r, f_s, f_r, a_s, a_r, c_s, c_r, s_s, s_r, hs_s, hs_r,
):
    t, z = lax.axis_index("tm"), lax.axis_index("space")
    core = lax.rem(t, 2)
    chip = t // 2
    mate = t + 1 - 2 * core
    per = 256 // chips
    low, high = z > 0, z < nz - 1

    ny, nx = (4, chips // 4) if chips >= 16 else (1, chips)
    offsets = sorted(
        ((dy, dx) for dy in range(ny) for dx in range(nx) if dy or dx),
        key=lambda o: -(min(o[0], ny - o[0]) + min(o[1], nx - o[1])),
    )

    def peer(o):
        return lax.rem(chip // nx + o[0], ny) * nx + lax.rem(lax.rem(chip, nx) + o[1], nx)

    def remote(src, dst, send, recv, tm, zz):
        return pltpu.make_async_remote_copy(
            src_ref=src, dst_ref=dst, send_sem=send, recv_sem=recv,
            device_id=(tm, zz), device_id_type=MESH,
        )

    barrier = pltpu.get_barrier_semaphore()

    def greet(tm, zz):
        pl.semaphore_signal(barrier, inc=1, device_id=(tm, zz), device_id_type=MESH)

    greet(mate, z)

    @pl.when(low)
    def _():
        greet(t, z - 1)

    @pl.when(high)
    def _():
        greet(t, z + 1)

    @pl.when(jnp.logical_and(low, core == 0))
    def _():
        greet(mate, z - 1)

    @pl.when(jnp.logical_and(high, core == 1))
    def _():
        greet(mate, z + 1)

    for o in offsets:
        greet(2 * peer(o) + core, z)

    load_x = pltpu.make_async_copy(x_hbm, xs, ld_sem.at[0])
    load_1 = pltpu.make_async_copy(w1_hbm, w1, ld_sem.at[1])
    load_2 = pltpu.make_async_copy(w2_hbm, w2, ld_sem.at[2])
    load_d = pltpu.make_async_copy(decay_hbm, rates.at[0], ld_sem.at[3])
    load_p = pltpu.make_async_copy(phase_hbm, rates.at[1], ld_sem.at[4])
    load_x.start()
    load_d.start()
    load_p.start()
    load_1.start()
    load_2.start()

    load_d.wait()
    load_p.wait()
    decay, phase = rates[0], rates[1]
    mag = jnp.exp(-decay)
    lam = (mag * jnp.cos(phase), mag * jnp.sin(phase))
    lam2 = times(lam, lam)
    factor = jnp.sqrt(1.0 - mag * mag) * SCALE
    factor = jnp.concatenate([factor, factor], axis=1)

    def base(half, i):
        pair = jnp.where(i == 3, 3, lax.rem(i + 1, 3))
        return jnp.where(half == 0, 2 * pair, 14 - 2 * pair)

    def spread(row, slot):
        v = row.astype(F32)
        at = lax.broadcasted_iota(jnp.int32, v.shape, 0)
        left = jnp.where(at == 0, 0.0, pltpu.roll(v, 1, 0))
        right = jnp.where(at == 127, 0.0, pltpu.roll(v, 127, 0))
        taps[slot, :, 0:256] = left.astype(BF16)
        taps[slot, :, 256:512] = row
        taps[slot, :, 512:768] = right.astype(BF16)

    def conv(w, row, other=None):
        acc = None
        for dy in range(3):
            if other is None:
                seen = taps[pl.ds(row + dy, 2)].reshape(256, 768)
            else:
                seen = jnp.concatenate([taps[row + dy], taps[other + dy]], axis=0)
            part = jnp.dot(seen, w[dy], preferred_element_type=F32)
            acc = part if acc is None else acc + part
        return acc

    def drive(i, between):
        @pl.loop(0, 2)
        def _(n):
            row = base(jnp.where(n == 0, 1 - core, core), i)
            f_own[pl.ds(row, 2)] = (conv(w1, row) * factor).reshape(2, 128, 256)

            @pl.when(n == 0)
            def _():
                between()
                feed_copy(i).start()

    def feed_copy(i):
        rows = pl.ds(base(1 - core, i), 2)
        return remote(f_own.at[rows], f_par.at[i], f_s.at[i], f_r.at[i], mate, z)

    def a_copy(i, d):
        j = peer(d)
        return remote(
            a_out.at[i, pl.ds(pl.multiple_of(j * per, per), per)], a_in.at[i, chip],
            a_s.at[i], a_r.at[i], 2 * j + core, z,
        )

    def a_all(i):
        blocks = a_in.at[i, pl.ds(0, chips - 1)]
        return remote(blocks, blocks, a_s.at[i], a_r.at[i], mate, z)

    def c_copy(i, d):
        j = peer(d)
        return remote(
            c_out.at[i, j], c_in.at[i, pl.ds(pl.multiple_of(chip * per, per), per)],
            c_s.at[i], c_r.at[i], 2 * j + core, z,
        )

    def c_all(i):
        blocks = c_in.at[i, pl.ds(0, (chips - 1) * per)]
        return remote(blocks, blocks, c_s.at[i], c_r.at[i], mate, z)

    def both_feeds(i, row, r, sub):
        mine = f_own[row + r, sub]
        other = f_par[i, r, sub]
        first = jnp.where(core == 0, mine, other)
        second = jnp.where(core == 0, other, mine)
        return (first[:, :128], first[:, 128:]), (second[:, :128], second[:, 128:])

    def aggregate(i):
        feed_copy(i).wait_recv()
        row = base(core, i)

        @pl.loop(0, 4)
        def _(n):
            r, q = n // 2, lax.rem(n, 2)
            sub = pl.ds(pl.multiple_of(q * 64, 64), 64)
            first, second = both_feeds(i, row, r, sub)
            total = plus(times(lam, first), second)
            out = pl.ds(pl.multiple_of(n * 64, 64), 64)
            a_out[i, out, 0:128] = encode(total[0])
            a_out[i, out, 128:256] = encode(total[1])

        for o in offsets:
            a_copy(i, o).start()

        a_in[i, chip] = a_out[i, pl.ds(pl.multiple_of(chip * per, per), per)]

    def scan(i):
        a_all(i).wait_recv()
        carry = (jnp.zeros((per, 128), F32), jnp.zeros((per, 128), F32))
        for k in range(chips):
            c_out[i, k, :, 0:128] = encode(carry[0])
            c_out[i, k, :, 128:256] = encode(carry[1])
            if k < chips - 1:
                got = (decode(a_in[i, k, :, 0:128]), decode(a_in[i, k, :, 128:256]))
                carry = plus(times(lam2, carry), got)

        for o in offsets:
            c_copy(i, o).start()

        c_in[i, pl.ds(pl.multiple_of(chip * per, per), per)] = c_out[i, chip]

    def mate_copy(i):
        rows = pl.ds(1 + base(core, i), 2)
        return remote(st_oth.at[i], st.at[rows], s_s.at[i], s_r.at[i], mate, z)

    def mate_landed(i):
        rows = pl.ds(1 + base(1 - core, i), 2)
        return remote(st.at[rows], st.at[rows], s_s.at[i], s_r.at[i], mate, z)

    def states(i):
        c_all(i).wait_recv()
        row = base(core, i)

        @pl.loop(0, 4)
        def _(n):
            r, q = n // 2, lax.rem(n, 2)
            sub = pl.ds(pl.multiple_of(q * 64, 64), 64)
            first, second = both_feeds(i, row, r, sub)
            took = pl.ds(pl.multiple_of(n * 64, 64), 64)
            carry = (decode(c_in[i, took, 0:128]), decode(c_in[i, took, 128:256]))
            s0 = plus(times(lam, carry), first)
            s1 = plus(times(lam, s0), second)
            for p in range(2):
                lanes = slice(128 * p, 128 * p + 128)
                own = jnp.where(core == 0, s0[p], s1[p]) * (1.0 / SCALE)
                oth = jnp.where(core == 0, s1[p], s0[p]) * (1.0 / SCALE)
                st[1 + row + r, sub, lanes] = own.astype(BF16)
                st_oth[i, r, sub, lanes] = oth.astype(BF16)

        mate_copy(i).start()

    def spread_states(half, i):
        row = base(half, i)

        @pl.loop(0, 2)
        def _(r):
            spread(st[1 + row + r], 1 + row + r)

    def gelu(mixed):
        return 0.5 * mixed * (1.0 + lax.erf(mixed * (0.5 ** 0.5)))

    def finish(row):
        out = gelu(conv(w2, row)).reshape(2, 128, 256)
        ov[pl.ds(row, 2)] = (xs[pl.ds(row, 2)].astype(F32) + out).astype(BF16)

    def finish_edges():
        out = gelu(conv(w2, 0, 15)).reshape(2, 128, 256)
        ov[0] = (xs[0].astype(F32) + out[0]).astype(BF16)
        ov[15] = (xs[15].astype(F32) + out[1]).astype(BF16)

    up = remote(xs.at[0], halo.at[1], hx_s.at[0], hx_r.at[1], t, z - 1)
    down = remote(xs.at[15], halo.at[0], hx_s.at[1], hx_r.at[0], t, z + 1)
    from_up = remote(halo.at[0], halo.at[0], hx_s.at[1], hx_r.at[0], t, z - 1)
    from_down = remote(halo.at[1], halo.at[1], hx_s.at[0], hx_r.at[1], t, z + 1)

    def meet():
        pl.semaphore_wait(
            barrier,
            chips + low.astype(jnp.int32) + high.astype(jnp.int32)
            + jnp.where(core == 0, low.astype(jnp.int32), high.astype(jnp.int32)),
        )

        @pl.when(low)
        def _():
            up.start()

        @pl.when(high)
        def _():
            down.start()

    def nothing():
        pass

    load_x.wait()

    @pl.loop(0, 8)
    def _(n):
        r = jnp.where(n < 4, 1 + n, 7 + n)
        spread(xs[r], 1 + r)

    load_1.wait()
    drive(0, meet)

    @pl.loop(0, 8)
    def _(n):
        r = lax.rem(jnp.where(n < 6, 5 + n, 9 + n), 16)
        spread(xs[r], 1 + r)

    drive(1, nothing)
    aggregate(0)

    def edges(first, second):
        @pl.when(low)
        def _():
            first()

        @pl.when(jnp.logical_not(low))
        def _():
            taps[0] = jnp.zeros((128, 768), BF16)

        @pl.when(high)
        def _():
            second()

        @pl.when(jnp.logical_not(high))
        def _():
            taps[17] = jnp.zeros((128, 768), BF16)

    def halo_first():
        from_up.wait_recv()
        spread(halo[0], 0)

    def halo_second():
        from_down.wait_recv()
        spread(halo[1], 17)

    edges(halo_first, halo_second)
    drive(2, nothing)
    aggregate(1)
    drive(3, nothing)
    aggregate(2)
    aggregate(3)

    @pl.loop(0, NC)
    def _(i):
        scan(i)

    own_up = remote(st.at[1], st.at[17], hs_s.at[0], hs_r.at[1], t, z - 1)
    oth_up = remote(st_oth.at[2, 0], st.at[17], hs_s.at[1], hs_r.at[1], mate, z - 1)
    own_down = remote(st.at[16], st.at[0], hs_s.at[0], hs_r.at[0], t, z + 1)
    oth_down = remote(st_oth.at[2, 1], st.at[0], hs_s.at[1], hs_r.at[0], mate, z + 1)
    state_up = remote(st.at[0], st.at[0], hs_s.at[0], hs_r.at[0], t, z - 1)
    state_down = remote(st.at[17], st.at[17], hs_s.at[0], hs_r.at[1], t, z + 1)
    sends_up = jnp.logical_and(core == 0, low)
    sends_down = jnp.logical_and(core == 1, high)

    def inner(half, row):
        return jnp.where(half == 0, row, 14 - row)

    def state_first():
        state_up.wait_recv()
        spread(st[0], 0)

    def state_second():
        state_down.wait_recv()
        spread(st[17], 17)

    load_2.wait()
    states(0)
    spread_states(core, 0)
    states(1)
    spread_states(core, 1)
    finish(inner(core, 3))
    mate_landed(0).wait_recv()
    spread_states(1 - core, 0)
    states(2)

    @pl.when(sends_up)
    def _():
        own_up.start()
        oth_up.start()

    @pl.when(sends_down)
    def _():
        own_down.start()
        oth_down.start()

    spread_states(core, 2)
    mate_landed(1).wait_recv()
    spread_states(1 - core, 1)
    finish(inner(1 - core, 3))
    finish(inner(core, 1))
    states(3)
    spread_states(core, 3)
    finish(inner(core, 5))
    mate_landed(2).wait_recv()
    spread_states(1 - core, 2)
    finish(inner(1 - core, 1))
    mate_landed(3).wait_recv()
    spread_states(1 - core, 3)
    finish(7)
    finish(inner(1 - core, 5))
    edges(state_first, state_second)
    finish_edges()

    @pl.when(low)
    def _():
        up.wait_send()

    @pl.when(high)
    def _():
        down.wait_send()

    @pl.when(sends_up)
    def _():
        own_up.wait_send()
        oth_up.wait_send()

    @pl.when(sends_down)
    def _():
        own_down.wait_send()
        oth_down.wait_send()

    @pl.loop(0, NC)
    def _(i):
        feed_copy(i).wait_send()
        mate_copy(i).wait_send()
        a_all(i).wait_send()
        c_all(i).wait_send()


def solution(mesh):
    chips, nz = mesh.shape["tm"] // 2, mesh.shape["space"]
    per = 256 // chips
    hbm_spec = pl.BlockSpec(memory_space=pltpu.HBM)
    vmem_spec = pl.BlockSpec(memory_space=pltpu.VMEM)
    dma = pltpu.SemaphoreType.DMA

    def on_device(frames_in, w_input, decay_rate, phase, w_output):
        out = pl.pallas_call(
            functools.partial(kernel, chips, nz),
            out_shape=pltpu.VMEM((16, 128, 256), BF16),
            in_specs=[hbm_spec] * 5,
            out_specs=vmem_spec,
            scratch_shapes=[
                pltpu.VMEM((16, 128, 256), BF16),
                pltpu.VMEM((3, 768, 256), BF16),
                pltpu.VMEM((3, 768, 256), BF16),
                pltpu.VMEM((2, 1, 128), F32),
                pltpu.VMEM((2, 128, 256), BF16),
                pltpu.VMEM((18, 128, 768), BF16),
                pltpu.VMEM((16, 128, 256), F32),
                pltpu.VMEM((NC, 2, 128, 256), F32),
                pltpu.VMEM((NC, 256, 256), BF16),
                pltpu.VMEM((NC, chips, per, 256), BF16),
                pltpu.VMEM((NC, chips, per, 256), BF16),
                pltpu.VMEM((NC, 256, 256), BF16),
                pltpu.VMEM((18, 128, 256), BF16),
                pltpu.VMEM((NC, 2, 128, 256), BF16),
                dma((5,)), dma((2,)), dma((2,)), dma((NC,)), dma((NC,)),
                dma((NC,)), dma((NC,)), dma((NC,)), dma((NC,)),
                dma((NC,)), dma((NC,)), dma((2,)), dma((2,)),
            ],
            compiler_params=pltpu.CompilerParams(
                collective_id=0, has_side_effects=True, vmem_limit_bytes=40 * 1024 * 1024
            ),
            name="convs5",
        )(
            *(pltpu.with_memory_space_constraint(v, pltpu.HBM) for v in (
            frames_in[0], w_input.reshape(3, 768, 256), w_output.reshape(3, 768, 256),
            decay_rate.reshape(1, 128), phase.reshape(1, 128)))
        )
        return out[None]

    in_specs = (P("tm", "space", None, None), P(), P(), P(), P())
    return jax.shard_map(
        on_device, mesh=mesh, in_specs=in_specs,
        out_specs=P("tm", "space", None, None), check_vma=False,
    )
```

```python
import functools

import jax
import jax.numpy as jnp
from jax import lax
from jax.experimental import pallas as pl
from jax.experimental.pallas import tpu as pltpu
from jax.sharding import PartitionSpec as P

MESH = pl.DeviceIdType.MESH
NC = 4
SCALE = 16384.0
TINY = 1.2e-38
F32 = jnp.float32
BF16 = jnp.bfloat16


def encode(v):
    return ((v * jnp.abs(v)) * (v * v)).astype(BF16)


def decode(code):
    w = code.astype(F32)
    size = jnp.abs(w)
    half = size * lax.rsqrt(jnp.maximum(size, TINY))
    root = half * lax.rsqrt(jnp.maximum(half, TINY))
    return jnp.where(w < 0, -root, root)


def times(a, b):
    return (a[0] * b[0] - a[1] * b[1], a[0] * b[1] + a[1] * b[0])


def plus(a, b):
    return (a[0] + b[0], a[1] + b[1])


def kernel(
    chips, nz,
    x_hbm, w1_hbm, w2_hbm, decay_hbm, phase_hbm,
    ov,
    xs, w1, w2, rates, halo, taps, f_own, f_par, a_out, a_in, c_out, c_in, st, st_oth,
    ld_sem, hx_s, hx_r, f_s, f_r, a_s, a_r, c_s, c_r, s_s, s_r, hs_s, hs_r,
):
    t, z = lax.axis_index("tm"), lax.axis_index("space")
    core = lax.rem(t, 2)
    chip = t // 2
    mate = t + 1 - 2 * core
    per = 256 // chips
    low, high = z > 0, z < nz - 1

    ny, nx = (4, chips // 4) if chips >= 16 else (1, chips)
    offsets = sorted(
        ((dy, dx) for dy in range(ny) for dx in range(nx) if dy or dx),
        key=lambda o: -(min(o[0], ny - o[0]) + min(o[1], nx - o[1])),
    )

    def peer(o):
        return lax.rem(chip // nx + o[0], ny) * nx + lax.rem(lax.rem(chip, nx) + o[1], nx)

    def remote(src, dst, send, recv, tm, zz):
        return pltpu.make_async_remote_copy(
            src_ref=src, dst_ref=dst, send_sem=send, recv_sem=recv,
            device_id=(tm, zz), device_id_type=MESH,
        )

    barrier = pltpu.get_barrier_semaphore()

    def greet(tm, zz):
        pl.semaphore_signal(barrier, inc=1, device_id=(tm, zz), device_id_type=MESH)

    greet(mate, z)

    @pl.when(low)
    def _():
        greet(t, z - 1)

    @pl.when(high)
    def _():
        greet(t, z + 1)

    @pl.when(jnp.logical_and(low, core == 0))
    def _():
        greet(mate, z - 1)

    @pl.when(jnp.logical_and(high, core == 1))
    def _():
        greet(mate, z + 1)

    for o in offsets:
        greet(2 * peer(o) + core, z)


    def load_rows(first, count, sem):
        rows = pl.ds(first, count)
        return pltpu.make_async_copy(x_hbm.at[rows], xs.at[rows], ld_sem.at[sem])

    load_a, load_b = load_rows(1, 4, 0), load_rows(11, 4, 5)
    load_rest = (load_rows(0, 1, 6), load_rows(15, 1, 7), load_rows(5, 6, 8))
    load_1 = [
        pltpu.make_async_copy(w1_hbm.at[dy], w1.at[dy], ld_sem.at[sem])
        for dy, sem in enumerate((1, 9, 10))
    ]
    load_2 = pltpu.make_async_copy(w2_hbm, w2, ld_sem.at[2])
    load_d = pltpu.make_async_copy(decay_hbm, rates.at[0], ld_sem.at[3])
    load_p = pltpu.make_async_copy(phase_hbm, rates.at[1], ld_sem.at[4])
    load_a.start()
    load_b.start()
    for copy in load_1:
        copy.start()
    load_d.start()
    load_p.start()
    for copy in load_rest:
        copy.start()

    load_d.wait()
    load_p.wait()
    decay, phase = rates[0], rates[1]
    mag = jnp.exp(-decay)
    lam = (mag * jnp.cos(phase), mag * jnp.sin(phase))
    lam2 = times(lam, lam)
    factor = jnp.sqrt(1.0 - mag * mag) * SCALE
    factor = jnp.concatenate([factor, factor], axis=1)

    def base(half, i):
        pair = jnp.where(i == 3, 3, lax.rem(i + 1, 3))
        return jnp.where(half == 0, 2 * pair, 14 - 2 * pair)

    def spread(row, slot):
        v = row.astype(F32)
        at = lax.broadcasted_iota(jnp.int32, v.shape, 0)
        left = jnp.where(at == 0, 0.0, pltpu.roll(v, 1, 0))
        right = jnp.where(at == 127, 0.0, pltpu.roll(v, 127, 0))
        taps[slot, :, 0:256] = left.astype(BF16)
        taps[slot, :, 256:512] = row
        taps[slot, :, 512:768] = right.astype(BF16)

    def conv(w, row, other=None, loads=None):
        acc = None
        for dy in range(3):
            if loads is not None:
                loads[dy].wait()
            if other is None:
                seen = taps[pl.ds(row + dy, 2)].reshape(256, 768)
            else:
                seen = jnp.concatenate([taps[row + dy], taps[other + dy]], axis=0)
            part = jnp.dot(seen, w[dy], preferred_element_type=F32)
            acc = part if acc is None else acc + part
        return acc

    def drive(half, i, loads=None):
        row = base(half, i)
        f_own[pl.ds(row, 2)] = (conv(w1, row, loads=loads) * factor).reshape(2, 128, 256)

    def feed_copy(i):
        rows = pl.ds(base(1 - core, i), 2)
        return remote(f_own.at[rows], f_par.at[i], f_s.at[0], f_r.at[i], mate, z)

    def a_copy(i, d):
        j = peer(d)
        return remote(
            a_out.at[i, pl.ds(pl.multiple_of(j * per, per), per)], a_in.at[i, chip],
            a_s.at[0], a_r.at[i], 2 * j + core, z,
        )

    def a_all(i):
        blocks = a_in.at[i, pl.ds(0, chips - 1)]
        return remote(blocks, blocks, a_s.at[0], a_r.at[i], mate, z)

    def c_copy(i, d):
        j = peer(d)
        return remote(
            c_out.at[i, j], c_in.at[i, pl.ds(pl.multiple_of(chip * per, per), per)],
            c_s.at[0], c_r.at[i], 2 * j + core, z,
        )

    def c_all(i):
        blocks = c_in.at[i, pl.ds(0, (chips - 1) * per)]
        return remote(blocks, blocks, c_s.at[0], c_r.at[i], mate, z)

    def both_feeds(i, row, r, sub):
        mine = f_own[row + r, sub]
        other = f_par[i, r, sub]
        first = jnp.where(core == 0, mine, other)
        second = jnp.where(core == 0, other, mine)
        return (first[:, :128], first[:, 128:]), (second[:, :128], second[:, 128:])

    def aggregate(i):
        feed_copy(i).wait_recv()
        row = base(core, i)

        @pl.loop(0, 4)
        def _(n):
            r, q = n // 2, lax.rem(n, 2)
            sub = pl.ds(pl.multiple_of(q * 64, 64), 64)
            first, second = both_feeds(i, row, r, sub)
            total = plus(times(lam, first), second)
            out = pl.ds(pl.multiple_of(n * 64, 64), 64)
            a_out[i, out, 0:128] = encode(total[0])
            a_out[i, out, 128:256] = encode(total[1])

        for o in offsets:
            a_copy(i, o).start()

        a_in[i, chip] = a_out[i, pl.ds(pl.multiple_of(chip * per, per), per)]

    def scan(i):
        a_all(i).wait_recv()
        carry = (jnp.zeros((per, 128), F32), jnp.zeros((per, 128), F32))
        for k in range(chips):
            c_out[i, k, :, 0:128] = encode(carry[0])
            c_out[i, k, :, 128:256] = encode(carry[1])
            if k < chips - 1:
                got = (decode(a_in[i, k, :, 0:128]), decode(a_in[i, k, :, 128:256]))
                carry = plus(times(lam2, carry), got)

        for o in offsets:
            c_copy(i, o).start()

        c_in[i, pl.ds(pl.multiple_of(chip * per, per), per)] = c_out[i, chip]

    def mate_copy(i):
        rows = pl.ds(1 + base(core, i), 2)
        return remote(st_oth.at[i], st.at[rows], s_s.at[0], s_r.at[i], mate, z)

    def mate_landed(i):
        rows = pl.ds(1 + base(1 - core, i), 2)
        return remote(st.at[rows], st.at[rows], s_s.at[0], s_r.at[i], mate, z)

    def states(i):
        c_all(i).wait_recv()
        row = base(core, i)

        @pl.loop(0, 4)
        def _(n):
            r, q = n // 2, lax.rem(n, 2)
            sub = pl.ds(pl.multiple_of(q * 64, 64), 64)
            first, second = both_feeds(i, row, r, sub)
            took = pl.ds(pl.multiple_of(n * 64, 64), 64)
            carry = (decode(c_in[i, took, 0:128]), decode(c_in[i, took, 128:256]))
            s0 = plus(times(lam, carry), first)
            s1 = plus(times(lam, s0), second)
            for p in range(2):
                lanes = slice(128 * p, 128 * p + 128)
                own = jnp.where(core == 0, s0[p], s1[p]) * (1.0 / SCALE)
                oth = jnp.where(core == 0, s1[p], s0[p]) * (1.0 / SCALE)
                st[1 + row + r, sub, lanes] = own.astype(BF16)
                st_oth[i, r, sub, lanes] = oth.astype(BF16)

        mate_copy(i).start()

    def spread_states(half, i):
        row = base(half, i)

        @pl.loop(0, 2)
        def _(r):
            spread(st[1 + row + r], 1 + row + r)

    def gelu(mixed):
        return 0.5 * mixed * (1.0 + lax.erf(mixed * (0.5 ** 0.5)))

    def finish(row):
        out = gelu(conv(w2, row)).reshape(2, 128, 256)
        ov[pl.ds(row, 2)] = (xs[pl.ds(row, 2)].astype(F32) + out).astype(BF16)

    def finish_edges():
        out = gelu(conv(w2, 0, 15)).reshape(2, 128, 256)
        ov[0] = (xs[0].astype(F32) + out[0]).astype(BF16)
        ov[15] = (xs[15].astype(F32) + out[1]).astype(BF16)

    up = remote(xs.at[0], halo.at[1], hx_s.at[0], hx_r.at[1], t, z - 1)
    down = remote(xs.at[15], halo.at[0], hx_s.at[1], hx_r.at[0], t, z + 1)
    from_up = remote(halo.at[0], halo.at[0], hx_s.at[1], hx_r.at[0], t, z - 1)
    from_down = remote(halo.at[1], halo.at[1], hx_s.at[0], hx_r.at[1], t, z + 1)

    def meet():
        pl.semaphore_wait(
            barrier,
            chips + low.astype(jnp.int32) + high.astype(jnp.int32)
            + jnp.where(core == 0, low.astype(jnp.int32), high.astype(jnp.int32)),
        )

        @pl.when(low)
        def _():
            up.start()

        @pl.when(high)
        def _():
            down.start()

    load_a.wait()
    load_b.wait()

    def edges(first, second):
        @pl.when(low)
        def _():
            first()

        @pl.when(jnp.logical_not(low))
        def _():
            taps[0] = jnp.zeros((128, 768), BF16)

        @pl.when(high)
        def _():
            second()

        @pl.when(jnp.logical_not(high))
        def _():
            taps[17] = jnp.zeros((128, 768), BF16)

    def halo_first():
        from_up.wait_recv()
        spread(halo[0], 0)

    def halo_second():
        from_down.wait_recv()
        spread(halo[1], 17)

    mate_half = 1 - core

    @pl.loop(0, 8)
    def _(n):
        r = jnp.where(n < 4, 1 + n, 7 + n)
        spread(xs[r], 1 + r)

    drive(mate_half, 0, load_1)
    load_2.start()
    for copy in load_rest:
        copy.wait()
    meet()
    feed_copy(0).start()
    drive(core, 0)

    @pl.loop(0, 4)
    def _(n):
        r = jnp.where(n < 2, 5 + n, 7 + n)
        spread(xs[r], 1 + r)

    drive(mate_half, 1)
    feed_copy(1).start()
    aggregate(0)

    @pl.loop(0, 4)
    def _(n):
        r = jnp.where(n < 2, 7 + n, 15 * (n - 2))
        spread(xs[r], 1 + r)

    drive(core, 1)
    drive(mate_half, 3)
    feed_copy(3).start()
    aggregate(1)
    drive(core, 3)
    edges(halo_first, halo_second)
    drive(mate_half, 2)
    feed_copy(2).start()
    aggregate(3)
    drive(core, 2)
    aggregate(2)

    for i in (0, 1, 3, 2):
        scan(i)

    own_up = remote(st.at[1], st.at[17], hs_s.at[0], hs_r.at[1], t, z - 1)
    oth_up = remote(st_oth.at[2, 0], st.at[17], hs_s.at[1], hs_r.at[1], mate, z - 1)
    own_down = remote(st.at[16], st.at[0], hs_s.at[0], hs_r.at[0], t, z + 1)
    oth_down = remote(st_oth.at[2, 1], st.at[0], hs_s.at[1], hs_r.at[0], mate, z + 1)
    state_up = remote(st.at[0], st.at[0], hs_s.at[0], hs_r.at[0], t, z - 1)
    state_down = remote(st.at[17], st.at[17], hs_s.at[0], hs_r.at[1], t, z + 1)
    sends_up = jnp.logical_and(core == 0, low)
    sends_down = jnp.logical_and(core == 1, high)

    def inner(half, row):
        return jnp.where(half == 0, row, 14 - row)

    def state_first():
        state_up.wait_recv()
        spread(st[0], 0)

    def state_second():
        state_down.wait_recv()
        spread(st[17], 17)

    load_2.wait()
    states(0)
    spread_states(core, 0)
    states(1)
    spread_states(core, 1)
    finish(inner(core, 3))
    mate_landed(0).wait_recv()
    spread_states(1 - core, 0)
    states(3)
    spread_states(core, 3)
    mate_landed(1).wait_recv()
    spread_states(1 - core, 1)
    finish(inner(core, 5))
    finish(inner(1 - core, 3))
    states(2)

    @pl.when(sends_up)
    def _():
        own_up.start()
        oth_up.start()

    @pl.when(sends_down)
    def _():
        own_down.start()
        oth_down.start()

    spread_states(core, 2)
    mate_landed(3).wait_recv()
    spread_states(1 - core, 3)
    finish(7)
    finish(inner(1 - core, 5))
    finish(inner(core, 1))
    mate_landed(2).wait_recv()
    spread_states(1 - core, 2)
    finish(inner(1 - core, 1))
    edges(state_first, state_second)
    finish_edges()

    @pl.when(low)
    def _():
        up.wait_send()

    @pl.when(high)
    def _():
        down.wait_send()

    @pl.when(sends_up)
    def _():
        own_up.wait_send()
        oth_up.wait_send()

    @pl.when(sends_down)
    def _():
        own_down.wait_send()
        oth_down.wait_send()

    blocks = a_in.at[:, pl.ds(0, chips - 1)]
    remote(f_par, f_par, f_s.at[0], f_r.at[0], mate, z).wait_send()
    remote(st_oth, st_oth, s_s.at[0], s_r.at[0], mate, z).wait_send()
    remote(blocks, blocks, a_s.at[0], a_r.at[0], mate, z).wait_send()
    remote(blocks, blocks, c_s.at[0], c_r.at[0], mate, z).wait_send()


def solution(mesh):
    chips, nz = mesh.shape["tm"] // 2, mesh.shape["space"]
    per = 256 // chips
    hbm_spec = pl.BlockSpec(memory_space=pltpu.HBM)
    vmem_spec = pl.BlockSpec(memory_space=pltpu.VMEM)
    dma = pltpu.SemaphoreType.DMA

    def on_device(frames_in, w_input, decay_rate, phase, w_output):
        out = pl.pallas_call(
            functools.partial(kernel, chips, nz),
            out_shape=pltpu.VMEM((16, 128, 256), BF16),
            in_specs=[hbm_spec] * 5,
            out_specs=vmem_spec,
            scratch_shapes=[
                pltpu.VMEM((16, 128, 256), BF16),
                pltpu.VMEM((3, 768, 256), BF16),
                pltpu.VMEM((3, 768, 256), BF16),
                pltpu.VMEM((2, 1, 128), F32),
                pltpu.VMEM((2, 128, 256), BF16),
                pltpu.VMEM((18, 128, 768), BF16),
                pltpu.VMEM((16, 128, 256), F32),
                pltpu.VMEM((NC, 2, 128, 256), F32),
                pltpu.VMEM((NC, 256, 256), BF16),
                pltpu.VMEM((NC, chips, per, 256), BF16),
                pltpu.VMEM((NC, chips, per, 256), BF16),
                pltpu.VMEM((NC, 256, 256), BF16),
                pltpu.VMEM((18, 128, 256), BF16),
                pltpu.VMEM((NC, 2, 128, 256), BF16),
                dma((11,)), dma((2,)), dma((2,)), dma((1,)), dma((NC,)),
                dma((1,)), dma((NC,)), dma((1,)), dma((NC,)),
                dma((1,)), dma((NC,)), dma((2,)), dma((2,)),
            ],
            compiler_params=pltpu.CompilerParams(
                collective_id=0, has_side_effects=True, vmem_limit_bytes=40 * 1024 * 1024
            ),
            name="convs5",
        )(
            *(pltpu.with_memory_space_constraint(v, pltpu.HBM) for v in (
            frames_in[0], w_input.reshape(3, 768, 256), w_output.reshape(3, 768, 256),
            decay_rate.reshape(1, 128), phase.reshape(1, 128)))
        )
        return out[None]

    in_specs = (P("tm", "space", None, None), P(), P(), P(), P())
    return jax.shard_map(
        on_device, mesh=mesh, in_specs=in_specs,
        out_specs=P("tm", "space", None, None), check_vma=False,
    )
```

```python
import functools

import jax
import jax.numpy as jnp
from jax import lax
from jax.experimental import pallas as pl
from jax.experimental.pallas import tpu as pltpu
from jax.sharding import PartitionSpec as P

MESH = pl.DeviceIdType.MESH
NC = 4
SCALE = 16384.0
TINY = 1.2e-38
F32 = jnp.float32
BF16 = jnp.bfloat16


def encode(v):
    return ((v * jnp.abs(v)) * (v * v)).astype(BF16)


def decode(code):
    w = code.astype(F32)
    size = jnp.abs(w)
    half = size * lax.rsqrt(jnp.maximum(size, TINY))
    root = half * lax.rsqrt(jnp.maximum(half, TINY))
    return jnp.where(w < 0, -root, root)


def times(a, b):
    return (a[0] * b[0] - a[1] * b[1], a[0] * b[1] + a[1] * b[0])


def plus(a, b):
    return (a[0] + b[0], a[1] + b[1])


def kernel(
    chips, nz,
    x_hbm, w1_hbm, w2_hbm, decay_hbm, phase_hbm,
    ov,
    xs, w1, w2, rates, halo, taps, f_own, f_par, a_out, a_in, c_out, c_in, st, st_oth, part,
    ld_sem, hx_s, hx_r, f_s, f_r, a_s, a_r, c_s, c_r, s_s, s_r, hs_s, hs_r,
):
    t, z = lax.axis_index("tm"), lax.axis_index("space")
    core = lax.rem(t, 2)
    chip = t // 2
    mate = t + 1 - 2 * core
    per = 256 // chips
    low, high = z > 0, z < nz - 1

    ny, nx = (4, chips // 4) if chips >= 16 else (1, chips)
    offsets = sorted(
        ((dy, dx) for dy in range(ny) for dx in range(nx) if dy or dx),
        key=lambda o: -(min(o[0], ny - o[0]) + min(o[1], nx - o[1])),
    )

    def peer(o):
        return lax.rem(chip // nx + o[0], ny) * nx + lax.rem(lax.rem(chip, nx) + o[1], nx)

    def remote(src, dst, send, recv, tm, zz):
        return pltpu.make_async_remote_copy(
            src_ref=src, dst_ref=dst, send_sem=send, recv_sem=recv,
            device_id=(tm, zz), device_id_type=MESH,
        )

    barrier = pltpu.get_barrier_semaphore()

    def greet(tm, zz):
        pl.semaphore_signal(barrier, inc=1, device_id=(tm, zz), device_id_type=MESH)

    for o in offsets:
        greet(2 * peer(o) + core, z)
    greet(mate, z)

    @pl.when(low)
    def _():
        greet(t, z - 1)

    @pl.when(high)
    def _():
        greet(t, z + 1)

    @pl.when(jnp.logical_and(low, core == 0))
    def _():
        greet(mate, z - 1)

    @pl.when(jnp.logical_and(high, core == 1))
    def _():
        greet(mate, z + 1)


    def load_rows(first, count, sem):
        rows = pl.ds(first, count)
        return pltpu.make_async_copy(x_hbm.at[rows], xs.at[rows], ld_sem.at[sem])

    load_a, load_b = load_rows(1, 4, 0), load_rows(11, 4, 5)
    load_rest = (load_rows(0, 1, 6), load_rows(15, 1, 7), load_rows(5, 6, 8))
    load_1 = [
        pltpu.make_async_copy(w1_hbm.at[dy], w1.at[dy], ld_sem.at[sem])
        for dy, sem in enumerate((1, 9, 10))
    ]
    load_2 = pltpu.make_async_copy(w2_hbm, w2, ld_sem.at[2])
    load_d = pltpu.make_async_copy(decay_hbm, rates.at[0], ld_sem.at[3])
    load_p = pltpu.make_async_copy(phase_hbm, rates.at[1], ld_sem.at[4])
    load_a.start()
    load_b.start()
    for copy in load_1:
        copy.start()
    load_d.start()
    load_p.start()
    for copy in load_rest:
        copy.start()

    load_d.wait()
    load_p.wait()
    decay, phase = rates[0], rates[1]
    mag = jnp.exp(-decay)
    lam = (mag * jnp.cos(phase), mag * jnp.sin(phase))
    lam2 = times(lam, lam)
    factor = jnp.sqrt(1.0 - mag * mag) * SCALE
    factor = jnp.concatenate([factor, factor], axis=1)

    def base(half, i):
        pair = jnp.where(i == 3, 3, lax.rem(i + 1, 3))
        return jnp.where(half == 0, 2 * pair, 14 - 2 * pair)

    def spread(row, slot):
        v = row.astype(F32)
        at = lax.broadcasted_iota(jnp.int32, v.shape, 0)
        left = jnp.where(at == 0, 0.0, pltpu.roll(v, 1, 0))
        right = jnp.where(at == 127, 0.0, pltpu.roll(v, 127, 0))
        taps[slot, :, 0:256] = left.astype(BF16)
        taps[slot, :, 256:512] = row
        taps[slot, :, 512:768] = right.astype(BF16)

    def conv(w, row, other=None, loads=None):
        acc = None
        for dy in range(3):
            if loads is not None:
                loads[dy].wait()
            if other is None:
                seen = taps[pl.ds(row + dy, 2)].reshape(256, 768)
            else:
                seen = jnp.concatenate([taps[row + dy], taps[other + dy]], axis=0)
            part = jnp.dot(seen, w[dy], preferred_element_type=F32)
            acc = part if acc is None else acc + part
        return acc

    def drive(half, i, loads=None):
        row = base(half, i)
        f_own[pl.ds(row, 2)] = (conv(w1, row, loads=loads) * factor).reshape(2, 128, 256)

    def feed_copy(i):
        rows = pl.ds(base(1 - core, i), 2)
        return remote(f_own.at[rows], f_par.at[i], f_s.at[0], f_r.at[i], mate, z)

    def a_copy(i, d):
        j = peer(d)
        return remote(
            a_out.at[i, pl.ds(pl.multiple_of(j * per, per), per)], a_in.at[i, chip],
            a_s.at[0], a_r.at[i], 2 * j + core, z,
        )

    def a_all(i):
        blocks = a_in.at[i, pl.ds(0, chips - 1)]
        return remote(blocks, blocks, a_s.at[0], a_r.at[i], mate, z)

    def c_copy(i, d):
        j = peer(d)
        return remote(
            c_out.at[i, j], c_in.at[i, pl.ds(pl.multiple_of(chip * per, per), per)],
            c_s.at[0], c_r.at[i], 2 * j + core, z,
        )

    def c_all(i):
        blocks = c_in.at[i, pl.ds(0, (chips - 1) * per)]
        return remote(blocks, blocks, c_s.at[0], c_r.at[i], mate, z)

    def both_feeds(i, row, r, sub):
        mine = f_own[row + r, sub]
        other = f_par[i, r, sub]
        first = jnp.where(core == 0, mine, other)
        second = jnp.where(core == 0, other, mine)
        return (first[:, :128], first[:, 128:]), (second[:, :128], second[:, 128:])

    def aggregate(i):
        feed_copy(i).wait_recv()
        row = base(core, i)

        @pl.loop(0, 4)
        def _(n):
            r, q = n // 2, lax.rem(n, 2)
            sub = pl.ds(pl.multiple_of(q * 64, 64), 64)
            first, second = both_feeds(i, row, r, sub)
            total = plus(times(lam, first), second)
            out = pl.ds(pl.multiple_of(n * 64, 64), 64)
            a_out[i, out, 0:128] = encode(total[0])
            a_out[i, out, 128:256] = encode(total[1])

        for o in offsets:
            a_copy(i, o).start()

        a_in[i, chip] = a_out[i, pl.ds(pl.multiple_of(chip * per, per), per)]

    def scan(i):
        a_all(i).wait_recv()
        carry = (jnp.zeros((per, 128), F32), jnp.zeros((per, 128), F32))
        for k in range(chips):
            c_out[i, k, :, 0:128] = encode(carry[0])
            c_out[i, k, :, 128:256] = encode(carry[1])
            if k < chips - 1:
                got = (decode(a_in[i, k, :, 0:128]), decode(a_in[i, k, :, 128:256]))
                carry = plus(times(lam2, carry), got)

        for o in offsets:
            c_copy(i, o).start()

        c_in[i, pl.ds(pl.multiple_of(chip * per, per), per)] = c_out[i, chip]

    def mate_copy(i):
        rows = pl.ds(1 + base(core, i), 2)
        return remote(st_oth.at[i], st.at[rows], s_s.at[0], s_r.at[i], mate, z)

    def mate_landed(i):
        rows = pl.ds(1 + base(1 - core, i), 2)
        return remote(st.at[rows], st.at[rows], s_s.at[0], s_r.at[i], mate, z)

    def states(i, after_edge=None):
        c_all(i).wait_recv()
        row = base(core, i)

        @pl.loop(0, 4)
        def _(step):
            n = step if after_edge is None else lax.rem(step + 2 * core, 4)
            r, q = n // 2, lax.rem(n, 2)
            sub = pl.ds(pl.multiple_of(q * 64, 64), 64)
            first, second = both_feeds(i, row, r, sub)
            took = pl.ds(pl.multiple_of(n * 64, 64), 64)
            carry = (decode(c_in[i, took, 0:128]), decode(c_in[i, took, 128:256]))
            s0 = plus(times(lam, carry), first)
            s1 = plus(times(lam, s0), second)
            for p in range(2):
                lanes = slice(128 * p, 128 * p + 128)
                own = jnp.where(core == 0, s0[p], s1[p]) * (1.0 / SCALE)
                oth = jnp.where(core == 0, s1[p], s0[p]) * (1.0 / SCALE)
                st[1 + row + r, sub, lanes] = own.astype(BF16)
                st_oth[i, r, sub, lanes] = oth.astype(BF16)

            if after_edge is not None:
                pl.when(step == 1)(after_edge)

        mate_copy(i).start()

    def spread_states(half, i):
        row = base(half, i)

        @pl.loop(0, 2)
        def _(r):
            spread(st[1 + row + r], 1 + row + r)

    def gelu(mixed):
        return 0.5 * mixed * (1.0 + lax.erf(mixed * (0.5 ** 0.5)))

    def finish(row):
        out = gelu(conv(w2, row)).reshape(2, 128, 256)
        ov[pl.ds(row, 2)] = (xs[pl.ds(row, 2)].astype(F32) + out).astype(BF16)

    def start_edges():
        for n, (row, taken) in enumerate(((0, (1, 2)), (15, (0, 1)))):
            acc = None
            for dy in taken:
                more = jnp.dot(taps[row + dy], w2[dy], preferred_element_type=F32)
                acc = more if acc is None else acc + more
            part[n] = acc

    def finish_edges():
        for n, (row, dy) in enumerate(((0, 0), (15, 2))):
            mixed = part[n] + jnp.dot(taps[row + dy], w2[dy], preferred_element_type=F32)
            ov[row] = (xs[row].astype(F32) + gelu(mixed)).astype(BF16)

    up = remote(xs.at[0], halo.at[1], hx_s.at[0], hx_r.at[1], t, z - 1)
    down = remote(xs.at[15], halo.at[0], hx_s.at[1], hx_r.at[0], t, z + 1)
    from_up = remote(halo.at[0], halo.at[0], hx_s.at[1], hx_r.at[0], t, z - 1)
    from_down = remote(halo.at[1], halo.at[1], hx_s.at[0], hx_r.at[1], t, z + 1)

    def meet():
        pl.semaphore_wait(
            barrier,
            chips + low.astype(jnp.int32) + high.astype(jnp.int32)
            + jnp.where(core == 0, low.astype(jnp.int32), high.astype(jnp.int32)),
        )

        @pl.when(low)
        def _():
            up.start()

        @pl.when(high)
        def _():
            down.start()

    load_a.wait()
    load_b.wait()

    def edges(first, second):
        @pl.when(low)
        def _():
            first()

        @pl.when(jnp.logical_not(low))
        def _():
            taps[0] = jnp.zeros((128, 768), BF16)

        @pl.when(high)
        def _():
            second()

        @pl.when(jnp.logical_not(high))
        def _():
            taps[17] = jnp.zeros((128, 768), BF16)

    def halo_first():
        from_up.wait_recv()
        spread(halo[0], 0)

    def halo_second():
        from_down.wait_recv()
        spread(halo[1], 17)

    mate_half = 1 - core

    @pl.loop(0, 8)
    def _(n):
        r = jnp.where(n < 4, 1 + n, 7 + n)
        spread(xs[r], 1 + r)

    drive(mate_half, 0, load_1)
    load_2.start()
    for copy in load_rest:
        copy.wait()
    meet()
    feed_copy(0).start()
    drive(core, 0)

    @pl.loop(0, 4)
    def _(n):
        r = jnp.where(n < 2, 5 + n, 7 + n)
        spread(xs[r], 1 + r)

    drive(mate_half, 1)
    feed_copy(1).start()
    aggregate(0)

    @pl.loop(0, 4)
    def _(n):
        r = jnp.where(n < 2, 7 + n, 15 * (n - 2))
        spread(xs[r], 1 + r)

    drive(core, 1)
    drive(mate_half, 3)
    feed_copy(3).start()
    aggregate(1)
    drive(core, 3)
    edges(halo_first, halo_second)
    drive(mate_half, 2)
    feed_copy(2).start()
    aggregate(3)
    drive(core, 2)
    aggregate(2)

    for i in (0, 1, 3, 2):
        scan(i)

    own_up = remote(st.at[1], st.at[17], hs_s.at[0], hs_r.at[1], t, z - 1)
    oth_up = remote(st_oth.at[2, 0], st.at[17], hs_s.at[1], hs_r.at[1], mate, z - 1)
    own_down = remote(st.at[16], st.at[0], hs_s.at[0], hs_r.at[0], t, z + 1)
    oth_down = remote(st_oth.at[2, 1], st.at[0], hs_s.at[1], hs_r.at[0], mate, z + 1)
    state_up = remote(st.at[0], st.at[0], hs_s.at[0], hs_r.at[0], t, z - 1)
    state_down = remote(st.at[17], st.at[17], hs_s.at[0], hs_r.at[1], t, z + 1)
    sends_up = jnp.logical_and(core == 0, low)
    sends_down = jnp.logical_and(core == 1, high)

    def inner(half, row):
        return jnp.where(half == 0, row, 14 - row)

    def send_edges():
        @pl.when(sends_up)
        def _():
            own_up.start()
            oth_up.start()

        @pl.when(sends_down)
        def _():
            own_down.start()
            oth_down.start()

    def state_first():
        state_up.wait_recv()
        spread(st[0], 0)

    def state_second():
        state_down.wait_recv()
        spread(st[17], 17)

    load_2.wait()
    states(0)
    spread_states(core, 0)
    states(1)
    spread_states(core, 1)
    finish(inner(core, 3))
    mate_landed(0).wait_recv()
    spread_states(1 - core, 0)
    states(3)
    spread_states(core, 3)
    mate_landed(1).wait_recv()
    spread_states(1 - core, 1)
    finish(inner(core, 5))
    finish(inner(1 - core, 3))
    states(2, send_edges)
    spread_states(core, 2)
    mate_landed(3).wait_recv()
    spread_states(1 - core, 3)
    finish(7)
    finish(inner(1 - core, 5))
    finish(inner(core, 1))
    mate_landed(2).wait_recv()
    spread_states(1 - core, 2)
    finish(inner(1 - core, 1))
    start_edges()
    edges(state_first, state_second)
    finish_edges()

    @pl.when(low)
    def _():
        up.wait_send()

    @pl.when(high)
    def _():
        down.wait_send()

    @pl.when(sends_up)
    def _():
        own_up.wait_send()
        oth_up.wait_send()

    @pl.when(sends_down)
    def _():
        own_down.wait_send()
        oth_down.wait_send()

    blocks = a_in.at[:, pl.ds(0, chips - 1)]
    remote(f_par, f_par, f_s.at[0], f_r.at[0], mate, z).wait_send()
    remote(st_oth, st_oth, s_s.at[0], s_r.at[0], mate, z).wait_send()
    remote(blocks, blocks, a_s.at[0], a_r.at[0], mate, z).wait_send()
    remote(blocks, blocks, c_s.at[0], c_r.at[0], mate, z).wait_send()


def solution(mesh):
    chips, nz = mesh.shape["tm"] // 2, mesh.shape["space"]
    per = 256 // chips
    hbm_spec = pl.BlockSpec(memory_space=pltpu.HBM)
    vmem_spec = pl.BlockSpec(memory_space=pltpu.VMEM)
    dma = pltpu.SemaphoreType.DMA

    def on_device(frames_in, w_input, decay_rate, phase, w_output):
        out = pl.pallas_call(
            functools.partial(kernel, chips, nz),
            out_shape=pltpu.VMEM((16, 128, 256), BF16),
            in_specs=[hbm_spec] * 5,
            out_specs=vmem_spec,
            scratch_shapes=[
                pltpu.VMEM((16, 128, 256), BF16),
                pltpu.VMEM((3, 768, 256), BF16),
                pltpu.VMEM((3, 768, 256), BF16),
                pltpu.VMEM((2, 1, 128), F32),
                pltpu.VMEM((2, 128, 256), BF16),
                pltpu.VMEM((18, 128, 768), BF16),
                pltpu.VMEM((16, 128, 256), F32),
                pltpu.VMEM((NC, 2, 128, 256), F32),
                pltpu.VMEM((NC, 256, 256), BF16),
                pltpu.VMEM((NC, chips, per, 256), BF16),
                pltpu.VMEM((NC, chips, per, 256), BF16),
                pltpu.VMEM((NC, 256, 256), BF16),
                pltpu.VMEM((18, 128, 256), BF16),
                pltpu.VMEM((NC, 2, 128, 256), BF16),
                pltpu.VMEM((2, 128, 256), F32),
                dma((11,)), dma((2,)), dma((2,)), dma((1,)), dma((NC,)),
                dma((1,)), dma((NC,)), dma((1,)), dma((NC,)),
                dma((1,)), dma((NC,)), dma((2,)), dma((2,)),
            ],
            compiler_params=pltpu.CompilerParams(
                collective_id=0, has_side_effects=True, vmem_limit_bytes=40 * 1024 * 1024
            ),
            name="convs5",
        )(
            *(pltpu.with_memory_space_constraint(v, pltpu.HBM) for v in (
            frames_in[0], w_input.reshape(3, 768, 256), w_output.reshape(3, 768, 256),
            decay_rate.reshape(1, 128), phase.reshape(1, 128)))
        )
        return out[None]

    in_specs = (P("tm", "space", None, None), P(), P(), P(), P())
    return jax.shard_map(
        on_device, mesh=mesh, in_specs=in_specs,
        out_specs=P("tm", "space", None, None), check_vma=False,
    )
```

```python
import functools

import jax
import jax.numpy as jnp
from jax import lax
from jax.experimental import pallas as pl
from jax.experimental.pallas import tpu as pltpu
from jax.sharding import PartitionSpec as P

MESH = pl.DeviceIdType.MESH
NC = 4
SCALE = 16384.0
TINY = 1.2e-38
F32 = jnp.float32
BF16 = jnp.bfloat16


def encode(v):
    return ((v * jnp.abs(v)) * (v * v)).astype(BF16)


def decode(code):
    w = code.astype(F32)
    size = jnp.abs(w)
    half = size * lax.rsqrt(jnp.maximum(size, TINY))
    root = half * lax.rsqrt(jnp.maximum(half, TINY))
    return jnp.where(w < 0, -root, root)


def times(a, b):
    return (a[0] * b[0] - a[1] * b[1], a[0] * b[1] + a[1] * b[0])


def plus(a, b):
    return (a[0] + b[0], a[1] + b[1])


def kernel(
    chips, nz,
    x_hbm, w1_hbm, w2_hbm, decay_hbm, phase_hbm,
    ov,
    xs, w1, w2, rates, halo, taps, f_own, f_par, a_out, a_in, c_out, c_in, st, st_oth, part,
    ld_sem, hx_s, hx_r, f_s, f_r, a_s, a_r, c_s, c_r, s_s, s_r, hs_s, hs_r,
):
    t, z = lax.axis_index("tm"), lax.axis_index("space")
    core = lax.rem(t, 2)
    chip = t // 2
    mate = t + 1 - 2 * core
    per = 256 // chips
    low, high = z > 0, z < nz - 1

    ny, nx = (4, chips // 4) if chips >= 16 else (1, chips)
    offsets = sorted(
        ((dy, dx) for dy in range(ny) for dx in range(nx) if dy or dx),
        key=lambda o: -(min(o[0], ny - o[0]) + min(o[1], nx - o[1])),
    )

    def peer(o):
        return lax.rem(chip // nx + o[0], ny) * nx + lax.rem(lax.rem(chip, nx) + o[1], nx)

    def remote(src, dst, send, recv, tm, zz):
        return pltpu.make_async_remote_copy(
            src_ref=src, dst_ref=dst, send_sem=send, recv_sem=recv,
            device_id=(tm, zz), device_id_type=MESH,
        )

    barrier = pltpu.get_barrier_semaphore()

    def greet(tm, zz):
        pl.semaphore_signal(barrier, inc=1, device_id=(tm, zz), device_id_type=MESH)

    for o in offsets:
        greet(2 * peer(o) + core, z)
    greet(mate, z)

    @pl.when(low)
    def _():
        greet(t, z - 1)

    @pl.when(high)
    def _():
        greet(t, z + 1)

    @pl.when(jnp.logical_and(low, core == 0))
    def _():
        greet(mate, z - 1)

    @pl.when(jnp.logical_and(high, core == 1))
    def _():
        greet(mate, z + 1)


    def load_rows(first, count, sem):
        rows = pl.ds(first, count)
        return pltpu.make_async_copy(x_hbm.at[rows], xs.at[rows], ld_sem.at[sem])

    load_a, load_b = load_rows(1, 4, 0), load_rows(11, 4, 5)
    load_rest = (load_rows(0, 1, 6), load_rows(15, 1, 7), load_rows(5, 6, 8))
    load_1 = [
        pltpu.make_async_copy(w1_hbm.at[dy], w1.at[dy], ld_sem.at[sem])
        for dy, sem in enumerate((1, 9, 10))
    ]
    load_2 = pltpu.make_async_copy(w2_hbm, w2, ld_sem.at[2])
    load_d = pltpu.make_async_copy(decay_hbm, rates.at[0], ld_sem.at[3])
    load_p = pltpu.make_async_copy(phase_hbm, rates.at[1], ld_sem.at[4])
    load_a.start()
    load_b.start()
    for copy in load_1:
        copy.start()
    load_d.start()
    load_p.start()
    for copy in load_rest:
        copy.start()

    load_d.wait()
    load_p.wait()
    decay, phase = rates[0], rates[1]
    mag = jnp.exp(-decay)
    lam = (mag * jnp.cos(phase), mag * jnp.sin(phase))
    lam2 = times(lam, lam)
    factor = jnp.sqrt(1.0 - mag * mag) * SCALE
    factor = jnp.concatenate([factor, factor], axis=1)

    def base(half, i):
        pair = jnp.where(i == 3, 3, lax.rem(i + 1, 3))
        return jnp.where(half == 0, 2 * pair, 14 - 2 * pair)

    def spread(row, slot):
        v = row.astype(F32)
        at = lax.broadcasted_iota(jnp.int32, v.shape, 0)
        left = jnp.where(at == 0, 0.0, pltpu.roll(v, 1, 0))
        right = jnp.where(at == 127, 0.0, pltpu.roll(v, 127, 0))
        taps[slot, :, 0:256] = left.astype(BF16)
        taps[slot, :, 256:512] = row
        taps[slot, :, 512:768] = right.astype(BF16)

    def conv(w, row, other=None, loads=None):
        acc = None
        for dy in range(3):
            if loads is not None:
                loads[dy].wait()
            if other is None:
                seen = taps[pl.ds(row + dy, 2)].reshape(256, 768)
            else:
                seen = jnp.concatenate([taps[row + dy], taps[other + dy]], axis=0)
            part = jnp.dot(seen, w[dy], preferred_element_type=F32)
            acc = part if acc is None else acc + part
        return acc

    def drive(half, i, loads=None):
        row = base(half, i)
        f_own[pl.ds(row, 2)] = (conv(w1, row, loads=loads) * factor).reshape(2, 128, 256)

    def feed_copy(i):
        rows = pl.ds(base(1 - core, i), 2)
        return remote(f_own.at[rows], f_par.at[i], f_s.at[0], f_r.at[i], mate, z)

    def a_copy(i, d):
        j = peer(d)
        return remote(
            a_out.at[i, pl.ds(pl.multiple_of(j * per, per), per)], a_in.at[i, chip],
            a_s.at[0], a_r.at[i], 2 * j + core, z,
        )

    def a_all(i):
        blocks = a_in.at[i, pl.ds(0, chips - 1)]
        return remote(blocks, blocks, a_s.at[0], a_r.at[i], mate, z)

    def c_copy(i, d):
        j = peer(d)
        return remote(
            c_out.at[i, j], c_in.at[i, pl.ds(pl.multiple_of(chip * per, per), per)],
            c_s.at[0], c_r.at[i], 2 * j + core, z,
        )

    def c_all(i):
        blocks = c_in.at[i, pl.ds(0, (chips - 1) * per)]
        return remote(blocks, blocks, c_s.at[0], c_r.at[i], mate, z)

    def both_feeds(i, row, r, sub):
        mine = f_own[row + r, sub]
        other = f_par[i, r, sub]
        first = jnp.where(core == 0, mine, other)
        second = jnp.where(core == 0, other, mine)
        return (first[:, :128], first[:, 128:]), (second[:, :128], second[:, 128:])

    def aggregate(i):
        feed_copy(i).wait_recv()
        row = base(core, i)

        @pl.loop(0, 4)
        def _(n):
            r, q = n // 2, lax.rem(n, 2)
            sub = pl.ds(pl.multiple_of(q * 64, 64), 64)
            first, second = both_feeds(i, row, r, sub)
            total = plus(times(lam, first), second)
            out = pl.ds(pl.multiple_of(n * 64, 64), 64)
            a_out[i, out, 0:128] = encode(total[0])
            a_out[i, out, 128:256] = encode(total[1])

        for o in offsets:
            a_copy(i, o).start()

        a_in[i, chip] = a_out[i, pl.ds(pl.multiple_of(chip * per, per), per)]

    def scan(i):
        a_all(i).wait_recv()
        carry = (jnp.zeros((per, 128), F32), jnp.zeros((per, 128), F32))
        for k in range(chips):
            c_out[i, k, :, 0:128] = encode(carry[0])
            c_out[i, k, :, 128:256] = encode(carry[1])
            if k < chips - 1:
                got = (decode(a_in[i, k, :, 0:128]), decode(a_in[i, k, :, 128:256]))
                carry = plus(times(lam2, carry), got)

        for o in offsets:
            c_copy(i, o).start()

        c_in[i, pl.ds(pl.multiple_of(chip * per, per), per)] = c_out[i, chip]

    def mate_copy(i):
        rows = pl.ds(1 + base(core, i), 2)
        return remote(st_oth.at[i], st.at[rows], s_s.at[0], s_r.at[i], mate, z)

    def mate_landed(i):
        rows = pl.ds(1 + base(1 - core, i), 2)
        return remote(st.at[rows], st.at[rows], s_s.at[0], s_r.at[i], mate, z)

    def states(i, after_edge=None):
        c_all(i).wait_recv()
        row = base(core, i)

        @pl.loop(0, 4)
        def _(step):
            n = step if after_edge is None else lax.rem(step + 2 * core, 4)
            r, q = n // 2, lax.rem(n, 2)
            sub = pl.ds(pl.multiple_of(q * 64, 64), 64)
            first, second = both_feeds(i, row, r, sub)
            took = pl.ds(pl.multiple_of(n * 64, 64), 64)
            carry = (decode(c_in[i, took, 0:128]), decode(c_in[i, took, 128:256]))
            s0 = plus(times(lam, carry), first)
            s1 = plus(times(lam, s0), second)
            for p in range(2):
                lanes = slice(128 * p, 128 * p + 128)
                own = jnp.where(core == 0, s0[p], s1[p]) * (1.0 / SCALE)
                oth = jnp.where(core == 0, s1[p], s0[p]) * (1.0 / SCALE)
                st[1 + row + r, sub, lanes] = own.astype(BF16)
                st_oth[i, r, sub, lanes] = oth.astype(BF16)

            if after_edge is not None:
                pl.when(step == 1)(after_edge)

        mate_copy(i).start()

    def spread_states(half, i):
        row = base(half, i)

        @pl.loop(0, 2)
        def _(r):
            spread(st[1 + row + r], 1 + row + r)

    def gelu(mixed):
        return 0.5 * mixed * (1.0 + lax.erf(mixed * (0.5 ** 0.5)))

    def finish(row):
        out = gelu(conv(w2, row)).reshape(2, 128, 256)
        ov[pl.ds(row, 2)] = (xs[pl.ds(row, 2)].astype(F32) + out).astype(BF16)

    def start_edges():
        for n, (row, taken) in enumerate(((0, (1, 2)), (15, (0, 1)))):
            acc = None
            for dy in taken:
                more = jnp.dot(taps[row + dy], w2[dy], preferred_element_type=F32)
                acc = more if acc is None else acc + more
            part[n] = acc

    def finish_edges():
        for n, (row, dy) in enumerate(((0, 0), (15, 2))):
            mixed = part[n] + jnp.dot(taps[row + dy], w2[dy], preferred_element_type=F32)
            ov[row] = (xs[row].astype(F32) + gelu(mixed)).astype(BF16)

    up = remote(xs.at[0], halo.at[1], hx_s.at[0], hx_r.at[1], t, z - 1)
    down = remote(xs.at[15], halo.at[0], hx_s.at[1], hx_r.at[0], t, z + 1)
    from_up = remote(halo.at[0], halo.at[0], hx_s.at[1], hx_r.at[0], t, z - 1)
    from_down = remote(halo.at[1], halo.at[1], hx_s.at[0], hx_r.at[1], t, z + 1)

    def meet():
        pl.semaphore_wait(
            barrier,
            chips + low.astype(jnp.int32) + high.astype(jnp.int32)
            + jnp.where(core == 0, low.astype(jnp.int32), high.astype(jnp.int32)),
        )

        @pl.when(low)
        def _():
            up.start()

        @pl.when(high)
        def _():
            down.start()

    load_a.wait()
    load_b.wait()

    def edges(first, second):
        @pl.when(low)
        def _():
            first()

        @pl.when(jnp.logical_not(low))
        def _():
            taps[0] = jnp.zeros((128, 768), BF16)

        @pl.when(high)
        def _():
            second()

        @pl.when(jnp.logical_not(high))
        def _():
            taps[17] = jnp.zeros((128, 768), BF16)

    def halo_first():
        from_up.wait_recv()
        spread(halo[0], 0)

    def halo_second():
        from_down.wait_recv()
        spread(halo[1], 17)

    mate_half = 1 - core

    @pl.loop(0, 8)
    def _(n):
        r = jnp.where(n < 4, 1 + n, 7 + n)
        spread(xs[r], 1 + r)

    drive(mate_half, 0, load_1)
    load_2.start()
    for copy in load_rest:
        copy.wait()

    @pl.loop(0, 4)
    def _(n):
        r = jnp.where(n < 2, 5 + n, 7 + n)
        spread(xs[r], 1 + r)

    meet()
    feed_copy(0).start()
    drive(core, 0)

    drive(mate_half, 1)
    feed_copy(1).start()
    aggregate(0)

    @pl.loop(0, 4)
    def _(n):
        r = jnp.where(n < 2, 7 + n, 15 * (n - 2))
        spread(xs[r], 1 + r)

    drive(core, 1)
    drive(mate_half, 3)
    feed_copy(3).start()
    aggregate(1)
    drive(core, 3)
    edges(halo_first, halo_second)
    drive(mate_half, 2)
    feed_copy(2).start()
    aggregate(3)
    drive(core, 2)
    aggregate(2)

    for i in (0, 1, 3, 2):
        scan(i)

    own_up = remote(st.at[1], st.at[17], hs_s.at[0], hs_r.at[1], t, z - 1)
    oth_up = remote(st_oth.at[2, 0], st.at[17], hs_s.at[1], hs_r.at[1], mate, z - 1)
    own_down = remote(st.at[16], st.at[0], hs_s.at[0], hs_r.at[0], t, z + 1)
    oth_down = remote(st_oth.at[2, 1], st.at[0], hs_s.at[1], hs_r.at[0], mate, z + 1)
    state_up = remote(st.at[0], st.at[0], hs_s.at[0], hs_r.at[0], t, z - 1)
    state_down = remote(st.at[17], st.at[17], hs_s.at[0], hs_r.at[1], t, z + 1)
    sends_up = jnp.logical_and(core == 0, low)
    sends_down = jnp.logical_and(core == 1, high)

    def inner(half, row):
        return jnp.where(half == 0, row, 14 - row)

    def send_edges():
        @pl.when(sends_up)
        def _():
            own_up.start()
            oth_up.start()

        @pl.when(sends_down)
        def _():
            own_down.start()
            oth_down.start()

    def state_first():
        state_up.wait_recv()
        spread(st[0], 0)

    def state_second():
        state_down.wait_recv()
        spread(st[17], 17)

    load_2.wait()
    states(0)
    spread_states(core, 0)
    states(1)
    spread_states(core, 1)
    finish(inner(core, 3))
    mate_landed(0).wait_recv()
    spread_states(1 - core, 0)
    states(3)
    spread_states(core, 3)
    mate_landed(1).wait_recv()
    spread_states(1 - core, 1)
    finish(inner(core, 5))
    finish(inner(1 - core, 3))
    states(2, send_edges)
    spread_states(core, 2)
    finish(inner(core, 1))
    mate_landed(3).wait_recv()
    spread_states(1 - core, 3)
    finish(7)
    finish(inner(1 - core, 5))
    mate_landed(2).wait_recv()
    spread_states(1 - core, 2)
    finish(inner(1 - core, 1))
    start_edges()
    edges(state_first, state_second)
    finish_edges()

    @pl.when(low)
    def _():
        up.wait_send()

    @pl.when(high)
    def _():
        down.wait_send()

    @pl.when(sends_up)
    def _():
        own_up.wait_send()
        oth_up.wait_send()

    @pl.when(sends_down)
    def _():
        own_down.wait_send()
        oth_down.wait_send()

    blocks = a_in.at[:, pl.ds(0, chips - 1)]
    remote(f_par, f_par, f_s.at[0], f_r.at[0], mate, z).wait_send()
    remote(st_oth, st_oth, s_s.at[0], s_r.at[0], mate, z).wait_send()
    remote(blocks, blocks, a_s.at[0], a_r.at[0], mate, z).wait_send()
    remote(blocks, blocks, c_s.at[0], c_r.at[0], mate, z).wait_send()


def solution(mesh):
    chips, nz = mesh.shape["tm"] // 2, mesh.shape["space"]
    per = 256 // chips
    hbm_spec = pl.BlockSpec(memory_space=pltpu.HBM)
    vmem_spec = pl.BlockSpec(memory_space=pltpu.VMEM)
    dma = pltpu.SemaphoreType.DMA

    def on_device(frames_in, w_input, decay_rate, phase, w_output):
        out = pl.pallas_call(
            functools.partial(kernel, chips, nz),
            out_shape=pltpu.VMEM((16, 128, 256), BF16),
            in_specs=[hbm_spec] * 5,
            out_specs=vmem_spec,
            scratch_shapes=[
                pltpu.VMEM((16, 128, 256), BF16),
                pltpu.VMEM((3, 768, 256), BF16),
                pltpu.VMEM((3, 768, 256), BF16),
                pltpu.VMEM((2, 1, 128), F32),
                pltpu.VMEM((2, 128, 256), BF16),
                pltpu.VMEM((18, 128, 768), BF16),
                pltpu.VMEM((16, 128, 256), F32),
                pltpu.VMEM((NC, 2, 128, 256), F32),
                pltpu.VMEM((NC, 256, 256), BF16),
                pltpu.VMEM((NC, chips, per, 256), BF16),
                pltpu.VMEM((NC, chips, per, 256), BF16),
                pltpu.VMEM((NC, 256, 256), BF16),
                pltpu.VMEM((18, 128, 256), BF16),
                pltpu.VMEM((NC, 2, 128, 256), BF16),
                pltpu.VMEM((2, 128, 256), F32),
                dma((11,)), dma((2,)), dma((2,)), dma((1,)), dma((NC,)),
                dma((1,)), dma((NC,)), dma((1,)), dma((NC,)),
                dma((1,)), dma((NC,)), dma((2,)), dma((2,)),
            ],
            compiler_params=pltpu.CompilerParams(
                collective_id=0, has_side_effects=True, vmem_limit_bytes=40 * 1024 * 1024
            ),
            name="convs5",
        )(
            *(pltpu.with_memory_space_constraint(v, pltpu.HBM) for v in (
            frames_in[0], w_input.reshape(3, 768, 256), w_output.reshape(3, 768, 256),
            decay_rate.reshape(1, 128), phase.reshape(1, 128)))
        )
        return out[None]

    in_specs = (P("tm", "space", None, None), P(), P(), P(), P())
    return jax.shard_map(
        on_device, mesh=mesh, in_specs=in_specs,
        out_specs=P("tm", "space", None, None), check_vma=False,
    )
```
